32 devices in a mesh: grid: 16 (over z, y, core), vec: 2 (over x).
Axes of the slice: x: 2, y: 2, z: 4, core: 2. Of those that a mesh axis runs over, the one named last changes fastest.
Arguments:
- tgt_coords: float32 [3, 2048], P(None, 'grid'), may hold values from 0 to 1
- src_coords: float32 [3, 2048], P(None, 'grid'), may hold values from 0 to 1
- src_values: float32 [2048, 2048], P('vec', 'grid'), may hold values from -0.53033006 to 0.53033006
- grad_vectors: float32 [3, 2048, 2048], P(None, 'vec', 'grid'), may hold values from -0.53033006 to 0.53033006
Outputs:
- interaction: float32 [2048, 2048], P('grid', 'vec')
The draws below stay inside these ranges and needn't reach their ends.
All inputs are finite; a program needn't handle non-finite values.
Results may differ from the reference program's by a relative error of at most 0.00023.
Values sent between devices are 32-bit elements; how exact they have to be, the bound alone decides.
A program may use at most 64 MiB of HBM per device.

```python
import math
import jax
import jax.numpy as jnp
from jax import lax

VECTORS = 2048
TARGETS = 2048
SOURCES = 2048


def raised(result, key, source, target, blocks, factor):
    def block_of(position):
        return (jnp.arange(result.shape[position]) // (result.shape[position] // blocks)).reshape((-1,) + (1,) * (result.ndim - 1 - position))

    one_side = jax.random.permutation(key, blocks)[block_of(target)]
    other_side = (block_of(target) + blocks // 2) % blocks
    return jnp.where((block_of(source) == one_side) | (block_of(source) == other_side), factor * result, result)


def block_levels(rng, extent, pieces, smallest, largest):
    factor_of = 1.0
    for dim, parts in pieces:
        draws = jax.random.uniform(jax.random.fold_in(jax.random.fold_in(rng, 6), dim), (parts,), jnp.float32, smallest / len(pieces), largest / len(pieces))
        factor_of = factor_of * jnp.repeat(jnp.exp(draws), extent[dim] // parts).reshape((-1,) + (1,) * (len(extent) - 1 - dim))
    return factor_of


def scatter_about(own_key, extent, width, reach, shards=(), held_as=jnp.bfloat16):
    result = width * jax.random.normal(own_key, extent, jnp.float32)
    if shards:
        result = result * block_levels(own_key, extent, shards, -0.22, 0.18)
    return jnp.clip(result, -reach, reach).astype(held_as)


def heavy_noise(rng, extent, width, bound, split, heavy, dtype=jnp.bfloat16):
    entries = width * jax.random.normal(rng, extent, jnp.float32)
    if split:
        entries = entries * block_levels(rng, extent, split, -0.22, 0.18)
    return jnp.clip(raised(entries, jax.random.fold_in(rng, 3), *heavy), -bound, bound).astype(dtype)


def setup_inputs(seed: int = 0) -> dict:
    keys = jax.random.split(jax.random.key(seed), 5)
    tgt_coords = jnp.clip(1.0 * jax.random.uniform(keys[0], (3, TARGETS), jnp.float32) ** block_levels(keys[0], (3, TARGETS), ((1, 16),), -0.2, 0.2), 0.0, 1.0)
    src_coords = jnp.clip(1.0 * jax.random.uniform(keys[1], (3, SOURCES), jnp.float32) ** block_levels(keys[1], (3, SOURCES), ((1, 16),), -0.2, 0.2), 0.0, 1.0)
    src_values = scatter_about(keys[2], (VECTORS, SOURCES), (4.0 * SOURCES ** -0.5), 0.53033006, ((0, 2), (1, 16)), jnp.float32)
    grad_vectors = heavy_noise(keys[3], (3, VECTORS, TARGETS), (4.0 * TARGETS ** -0.5), 0.53033006, ((1, 2), (2, 16)), (2, 1, 16, 2.0), jnp.float32)
    return {"tgt_coords": tgt_coords, "src_coords": src_coords, "src_values": src_values, "grad_vectors": grad_vectors}


stiff = 1.0
soft = 0.05

def pair_kernel(targets, sources):
    diff = targets[:, :, None] - sources[:, None, :]
    dist2 = lax.optimization_barrier(jnp.sum(diff * diff, axis=0))
    scale = 0.5 / ((1.0 + stiff * jnp.sqrt(dist2)) ** 2 * jnp.sqrt(dist2 + soft * soft))
    return diff * scale[None, :, :]

def reference(tgt_coords, src_coords, src_values, grad_vectors):
    block_len = math.gcd(TARGETS, 512)
    nblocks = TARGETS // block_len
    tgt_blocks = tgt_coords.reshape(3, nblocks, block_len).transpose(1, 0, 2)
    grad_blocks = grad_vectors.reshape(3, VECTORS, nblocks, block_len).transpose(2, 0, 1, 3)

    def step(total, items):
        tblock, gblock = items
        kern = pair_kernel(tblock, src_coords)
        partial_y = jnp.einsum('cts,qs->ctq', kern, src_values, precision=lax.Precision.HIGHEST)
        total = total + jnp.einsum('cpt,ctq->pq', gblock, partial_y, precision=lax.Precision.HIGHEST)
        return (total, None)
    total, _ = lax.scan(step, jnp.zeros((VECTORS, VECTORS), jnp.float32), (tgt_blocks, grad_blocks))
    return total
```

```python
import functools

import jax
import jax.numpy as jnp
from jax import lax
from jax.experimental import pallas as pl
from jax.experimental.pallas import tpu as pltpu
from jax.sharding import PartitionSpec as P

stiff = 1.0
soft = 0.05
MESH = pl.DeviceIdType.MESH
ROWS = 16
K_BYTES = 16 << 20


def split(value):
    high = value.astype(jnp.bfloat16)
    low = (value - high.astype(jnp.float32)).astype(jnp.bfloat16)
    return high, low


def dot3(ah, al, bh, bl, dims):
    dot = functools.partial(lax.dot_general, dimension_numbers=(dims, ((), ())), preferred_element_type=jnp.float32)
    return dot(ah, bh) + (dot(ah, bl) + dot(al, bh))


def kernel(sizes, coord_ref, v_ref, g_ref, out_ref,
           cbuf, tcol, gbuf, gh, gl, vbuf, vh, vl, kh, kl, zpart, zbuf, zall, ipart, ibuf,
           csend, crecv, gsend, grecv, vsend, vrecv, zsend, zrecv, xsend, xrecv, isend, irecv):
    A, B, m, nb, R, T, S, slots = sizes
    n = A * B
    me, mv = lax.axis_index("grid"), lax.axis_index("vec")
    ma, mb = me // B, me % B

    barrier = pltpu.get_barrier_semaphore()
    for k in range(1, n):
        pl.semaphore_signal(barrier, inc=1, device_id={"grid": lax.rem(me + k, n)}, device_id_type=MESH)
    for k in range(1, m):
        pl.semaphore_signal(barrier, inc=1, device_id={"vec": lax.rem(mv + k, m)}, device_id_type=MESH)
    pl.semaphore_wait(barrier, n - 1 + m - 1)

    def remote(src, dst, send, recv, device):
        return pltpu.make_async_remote_copy(
            src_ref=src, dst_ref=dst, send_sem=send, recv_sem=recv, device_id=device, device_id_type=MESH)

    def coord_copy(k):
        return remote(coord_ref, cbuf.at[me], csend.at[k], crecv.at[me], {"grid": lax.rem(me + k, n)})

    def coord_arrival(k):
        o = lax.rem(me + k, n)
        return remote(coord_ref, cbuf.at[o], csend.at[k], crecv.at[o], {"grid": o})

    def b_peer(k):
        return lax.rem(mb + k, B)

    def g_copy(k):
        o = b_peer(k)
        return remote(g_ref.at[:, :, o], gbuf.at[mb], gsend.at[k], grecv.at[mb], {"grid": ma * B + o})

    def g_arrival(k):
        o = b_peer(k)
        return remote(gbuf.at[o], gbuf.at[o], gsend.at[k], grecv.at[o], {"grid": ma * B + o})

    def v_copy(k):
        return remote(v_ref, vbuf.at[mb], vsend.at[k], vrecv.at[mb], {"grid": ma * B + b_peer(k)})

    def v_arrival(k):
        o = b_peer(k)
        return remote(v_ref, vbuf.at[o], vsend.at[k], vrecv.at[o], {"grid": ma * B + o})

    def z_copy(k):
        o = lax.rem(ma + k, A)
        return remote(zpart.at[k - 1], zbuf.at[ma], zsend.at[k], zrecv.at[ma], {"grid": o * B + mb})

    def z_arrival(k):
        o = lax.rem(ma + k, A)
        return remote(zbuf.at[o], zbuf.at[o], zsend.at[k], zrecv.at[o], {"grid": o * B + mb})

    def x_copy(k):
        return remote(zall.at[mv], zall.at[mv], xsend.at[k], xrecv.at[mv], {"vec": lax.rem(mv + k, m)})

    def x_arrival(k):
        o = lax.rem(mv + k, m)
        return remote(zall.at[o], zall.at[o], xsend.at[k], xrecv.at[o], {"vec": o})

    def i_copy(o):
        return remote(ipart.at[o], ibuf.at[ma], isend.at[o], irecv.at[ma], {"grid": o * B + mb})

    def i_arrival(k):
        o = lax.rem(ma + k, A)
        return remote(ibuf.at[o], ibuf.at[o], isend.at[o], irecv.at[o], {"grid": o * B + mb})

    for k in range(1, n):
        coord_copy(k).start()
    for k in range(1, B):
        g_copy(k).start()

    cbuf[me] = coord_ref[...]
    gbuf[mb] = g_ref[:, :, mb]
    vbuf[mb] = v_ref[...]

    for k in range(1, n):
        coord_arrival(k).wait_recv()

    for j in range(B):
        for c in range(3):
            row = cbuf[ma * B + j, 3 + c:4 + c, :]
            tcol[c, j * T:(j + 1) * T, :] = jnp.broadcast_to(row, (S, T)).T

    def make_pair_kernel(k, slot):
        block = lax.rem(ma + k, A)
        for j in range(B):
            def rows(i, carry, j=j):
                start = pl.multiple_of(i * ROWS, ROWS)
                at = j * T + start
                tx, ty, tz = (tcol[c, pl.ds(pl.multiple_of(at, ROWS), ROWS), :] for c in range(3))
                for q in range(B):
                    src = block * B + q
                    diff = [t - jnp.broadcast_to(cbuf[src, c:c + 1, :], (ROWS, S)) for c, t in enumerate((tx, ty, tz))]
                    dist2 = diff[0] * diff[0] + diff[1] * diff[1] + diff[2] * diff[2]
                    near = 1.0 + stiff * jnp.sqrt(dist2)
                    scale = 0.5 / (near * near * jnp.sqrt(dist2 + soft * soft))
                    for c in range(3):
                        high, low = split(diff[c] * scale)
                        where = pl.ds(pl.multiple_of((j * 3 + c) * T + start, ROWS), ROWS)
                        kh[slot, where, q * S:(q + 1) * S] = high
                        kl[slot, where, q * S:(q + 1) * S] = low
                return carry
            lax.fori_loop(0, T // ROWS, rows, 0)

    order = list(range(1, A)) + [0]
    for slot in range(slots):
        make_pair_kernel(order[slot], slot)

    for k in range(1, B):
        g_arrival(k).wait_recv()
    for k in range(1, B):
        v_copy(k).start()
    for j in range(B):
        for c in range(3):
            for zz in range(nb):
                high, low = split(gbuf[j, c, zz])
                gh[zz * R:(zz + 1) * R, (j * 3 + c) * T:(j * 3 + c + 1) * T] = high
                gl[zz * R:(zz + 1) * R, (j * 3 + c) * T:(j * 3 + c + 1) * T] = low

    for step, k in enumerate(order):
        slot = step % slots
        if step >= slots:
            make_pair_kernel(k, slot)
        zpart[k - 1 if k else A - 1] = dot3(gh[...], gl[...], kh[slot], kl[slot], ((1,), (0,)))
        if k:
            z_copy(k).start()

    for k in range(1, B):
        v_arrival(k).wait_recv()
    for j in range(B):
        high, low = split(vbuf[j])
        vh[:, j * S:(j + 1) * S] = high
        vl[:, j * S:(j + 1) * S] = low

    total = zpart[A - 1]
    for k in range(1, A):
        z_arrival(k).wait_recv()
        total = total + zbuf[lax.rem(ma + k, A)]
    zall[mv] = total
    for k in range(1, m):
        x_copy(k).start()

    for k in range(m):
        slab = lax.rem(mv + k, m)
        if k:
            x_arrival(k).wait_recv()
        for zz in range(nb):
            o = slab * nb + zz
            zh, zl = split(zall[slab, zz * R:(zz + 1) * R, :])
            ipart[o] = dot3(zh, zl, vh[...], vl[...], ((1,), (1,)))

            @pl.when(o != ma)
            def _(o=o):
                i_copy(o).start()

    total = ipart[ma]
    for k in range(1, A):
        i_arrival(k).wait_recv()
        total = total + ibuf[lax.rem(ma + k, A)]
    out_ref[...] = total

    for k in range(1, n):
        coord_copy(k).wait_send()
    for k in range(1, B):
        g_copy(k).wait_send()
        v_copy(k).wait_send()
    for k in range(1, A):
        z_copy(k).wait_send()
        i_copy(lax.rem(ma + k, A)).wait_send()
    for k in range(1, m):
        x_copy(k).wait_send()


def solution(mesh):
    n, m = mesh.shape["grid"], mesh.shape["vec"]
    A = min((d for d in range(m, n + 1, m) if n % d == 0), key=lambda d: abs(d - n // d))
    B, nb = n // A, A // m

    def body(tgt_coords, src_coords, src_values, grad_vectors):
        T, S = tgt_coords.shape[1], src_coords.shape[1]
        Q, slab = src_values.shape[0], grad_vectors.shape[1]
        R = slab * m // n
        f32, bf16 = jnp.float32, jnp.bfloat16
        coords = jnp.concatenate([src_coords, tgt_coords, jnp.zeros((2, S), f32)], axis=0)
        grads = grad_vectors.reshape(3, nb, B, R, T)
        depth, width = 3 * B * T, B * S
        slots = max(1, min(A, K_BYTES // (depth * width * 4)))
        V, DMA = pltpu.VMEM, pltpu.SemaphoreType.DMA
        return pl.pallas_call(
            functools.partial(kernel, (A, B, m, nb, R, T, S, slots)),
            out_shape=jax.ShapeDtypeStruct((R, Q), f32),
            in_specs=[pl.BlockSpec(memory_space=pltpu.VMEM)] * 3,
            out_specs=pl.BlockSpec(memory_space=pltpu.VMEM),
            scratch_shapes=[
                V((n, 8, S), f32), V((3, B * T, S), f32),
                V((B, 3, nb, R, T), f32), V((nb * R, depth), bf16), V((nb * R, depth), bf16),
                V((B, Q, S), f32), V((Q, width), bf16), V((Q, width), bf16),
                V((slots, depth, width), bf16), V((slots, depth, width), bf16),
                V((A, nb * R, width), f32), V((A, nb * R, width), f32), V((m, nb * R, width), f32),
                V((A, R, Q), f32), V((A, R, Q), f32),
                DMA((n,)), DMA((n,)), DMA((B,)), DMA((B,)), DMA((B,)), DMA((B,)),
                DMA((A,)), DMA((A,)), DMA((m,)), DMA((m,)), DMA((A,)), DMA((A,)),
            ],
            compiler_params=pltpu.CompilerParams(
                collective_id=0, has_side_effects=True, vmem_limit_bytes=56 << 20),
        )(coords, src_values, grads)

    return jax.shard_map(
        body,
        mesh=mesh,
        in_specs=(P(None, "grid"), P(None, "grid"), P("vec", "grid"), P(None, "vec", "grid")),
        out_specs=P("grid", "vec"),
        check_vma=False,
    )
```

```python
import functools

import jax
import jax.numpy as jnp
from jax import lax
from jax.experimental import pallas as pl
from jax.experimental.pallas import tpu as pltpu
from jax.sharding import PartitionSpec as P

stiff = 1.0
soft = 0.05
MESH = pl.DeviceIdType.MESH
ROWS = 16
K_BYTES = 16 << 20


def split(value):
    high = value.astype(jnp.bfloat16)
    low = (value - high.astype(jnp.float32)).astype(jnp.bfloat16)
    return high, low


def dot3(ah, al, bh, bl, dims):
    dot = functools.partial(lax.dot_general, dimension_numbers=(dims, ((), ())), preferred_element_type=jnp.float32)
    return dot(ah, bh) + (dot(ah, bl) + dot(al, bh))


def kernel(sizes, coord_ref, v_ref, g_ref, out_ref,
           cbuf, tcol, gbuf, gh, gl, vbuf, vh, vl, kh, kl, zpart, zup, zdown, zall, ipart, iup, idown,
           csend, crecv, gsend, grecv, vsend, vrecv, zsend, zuprecv, zdownrecv, xsend, xrecv,
           isend, iuprecv, idownrecv):
    A, B, m, nb, R, T, S, H, slots = sizes
    n = A * B
    me, mv = lax.axis_index("grid"), lax.axis_index("vec")
    ma, mb = me // B, me % B

    barrier = pltpu.get_barrier_semaphore()
    for k in range(1, n):
        pl.semaphore_signal(barrier, inc=1, device_id={"grid": lax.rem(me + k, n)}, device_id_type=MESH)
    for k in range(1, m):
        pl.semaphore_signal(barrier, inc=1, device_id={"vec": lax.rem(mv + k, m)}, device_id_type=MESH)
    pl.semaphore_wait(barrier, n - 1 + m - 1)

    def remote(src, dst, send, recv, device):
        return pltpu.make_async_remote_copy(
            src_ref=src, dst_ref=dst, send_sem=send, recv_sem=recv, device_id=device, device_id_type=MESH)

    def coord_copy(k):
        return remote(coord_ref, cbuf.at[me], csend.at[k], crecv.at[me], {"grid": lax.rem(me + k, n)})

    def coord_arrival(k):
        o = lax.rem(me + k, n)
        return remote(coord_ref, cbuf.at[o], csend.at[k], crecv.at[o], {"grid": o})

    def b_peer(k):
        return lax.rem(mb + k, B)

    def row_block(e, slab):
        return jnp.where(2 * slab < m, e, nb - 1 - e)

    def g_copy(e, k):
        o = b_peer(k)
        return remote(g_ref.at[:, row_block(e, mv), o], gbuf.at[e, mb], gsend.at[e, k], grecv.at[e, mb],
                      {"grid": ma * B + o})

    def g_arrival(e, k):
        o = b_peer(k)
        return remote(gbuf.at[e, o], gbuf.at[e, o], gsend.at[e, k], grecv.at[e, o], {"grid": ma * B + o})

    twin = mb + 1 - 2 * lax.rem(mb, 2)

    def v_copy(k):
        return remote(v_ref, vbuf.at[mb], vsend.at[k], vrecv.at[mb], {"grid": ma * B + b_peer(k)})

    def v_pass(k):
        o = b_peer(k)
        return remote(vbuf.at[o], vbuf.at[o], vsend.at[k + 1], vrecv.at[o], {"grid": ma * B + twin})

    def v_own():
        return remote(v_ref, vbuf.at[mb], vsend.at[0], vrecv.at[mb], {"grid": ma * B + twin})

    def v_arrival(o):
        return remote(v_ref, vbuf.at[o], vsend.at[0], vrecv.at[o], {"grid": ma * B + twin})

    def z_copy(e, o, up):
        buf, recv, to = (zup, zuprecv, ma + 1) if up else (zdown, zdownrecv, ma - 1)
        return remote(zpart.at[e, o], buf.at[e, o], zsend.at[e, o], recv.at[e, o],
                      {"grid": lax.rem(to + A, A) * B + mb})

    def x_copy(e, k):
        return remote(zall.at[e, mv], zall.at[e, mv], xsend.at[e, k], xrecv.at[e, mv], {"vec": lax.rem(mv + k, m)})

    def x_arrival(e, k):
        o = lax.rem(mv + k, m)
        return remote(zall.at[e, o], zall.at[e, o], xsend.at[e, k], xrecv.at[e, o], {"vec": o})

    def i_copy(h, o, up):
        buf, recv, to = (iup, iuprecv, ma + 1) if up else (idown, idownrecv, ma - 1)
        return remote(ipart.at[h, o], buf.at[h, o], isend.at[h, o], recv.at[h, o],
                      {"grid": lax.rem(to + A, A) * B + mb})

    def inward(blocks):
        for u, d in zip(sorted(blocks, reverse=True), sorted(blocks)):
            yield u, True
            yield d, False

    for k in range(1, n):
        coord_copy(k).start()
    for e in range(nb):
        for k in range(1, B):
            g_copy(e, k).start()

    cbuf[me] = coord_ref[...]
    for e in range(nb):
        gbuf[e, mb] = g_ref[:, row_block(e, mv), mb]
    vbuf[mb] = v_ref[...]

    for k in range(1, n):
        coord_arrival(k).wait_recv()

    for j in range(B):
        for c in range(3):
            row = cbuf[ma * B + j, 3 + c:4 + c, :]
            tcol[c, j * T:(j + 1) * T, :] = jnp.broadcast_to(row, (S, T)).T

    def make_pair_kernel(block, slot):
        def rows(i, carry):
            j, start = i // (T // ROWS), i % (T // ROWS) * ROWS
            at = pl.ds(pl.multiple_of(i * ROWS, ROWS), ROWS)
            txyz = [tcol[c, at, :] for c in range(3)]
            for q in range(B):
                src = block * B + q
                diff = [t - jnp.broadcast_to(cbuf[src, c:c + 1, :], (ROWS, S)) for c, t in enumerate(txyz)]
                dist2 = diff[0] * diff[0] + diff[1] * diff[1] + diff[2] * diff[2]
                near = 1.0 + stiff * jnp.sqrt(dist2)
                scale = 0.5 / (near * near * jnp.sqrt(dist2 + soft * soft))
                for c in range(3):
                    high, low = split(diff[c] * scale)
                    where = pl.ds(pl.multiple_of((j * 3 + c) * T + start, ROWS), ROWS)
                    kh[slot, where, q * S:(q + 1) * S] = high
                    kl[slot, where, q * S:(q + 1) * S] = low
            return carry
        lax.fori_loop(0, B * T // ROWS, rows, 0)

    order = []
    for u, d in zip(range(A - 1, -1, -1), range(A)):
        order += [o for o in (u, d) if o not in order]
    for slot in range(slots):
        make_pair_kernel(order[slot], slot)

    def z_parts(e):
        for k in range(1, B):
            g_arrival(e, k).wait_recv()
        for j in range(B):
            for c in range(3):
                high, low = split(gbuf[e, j, c])
                gh[:, (j * 3 + c) * T:(j * 3 + c + 1) * T] = high
                gl[:, (j * 3 + c) * T:(j * 3 + c + 1) * T] = low
        for step, o in enumerate(order):
            slot = step % slots
            if slots < A and (e or step >= slots):
                make_pair_kernel(o, slot)
            zpart[e, o] = dot3(gh[...], gl[...], kh[slot], kl[slot], ((1,), (0,)))

            @pl.when(jnp.logical_and(ma == 0, o > 0))
            def _():
                z_copy(e, o, True).start()

            @pl.when(jnp.logical_and(ma == A - 1, o < A - 1))
            def _():
                z_copy(e, o, False).start()

    def z_relay(e):
        for o, up in inward(range(A)):
            inner, first = (ma < o, ma > 0) if up else (ma > o, ma < A - 1)

            @pl.when(jnp.logical_and(inner, first))
            def _(o=o, up=up):
                z_copy(e, o, up).wait_recv()
                zpart[e, o] = zpart[e, o] + (zup if up else zdown)[e, o]
                z_copy(e, o, up).start()

    def own_sum(copy, part, upbuf, downbuf, h):
        @pl.when(ma > 0)
        def _():
            copy(h, ma, True).wait_recv()
            part[h, ma] = part[h, ma] + upbuf[h, ma]

        @pl.when(ma < A - 1)
        def _():
            copy(h, ma, False).wait_recv()
            part[h, ma] = part[h, ma] + downbuf[h, ma]
        return part[h, ma]

    def z_sum(e):
        zall[e, mv] = own_sum(z_copy, zpart, zup, zdown, e)
        for k in range(1, m):
            x_copy(e, k).start()

    def i_parts(e):
        for k in range(1, m):
            x_arrival(e, k).wait_recv()
        blocks = {slab * nb + (e if 2 * slab < m else nb - 1 - e): slab for slab in range(m)}
        W = vh.shape[0] // H
        for o in sorted(blocks, key=order.index):
            zh, zl = split(zall[e, blocks[o]])
            for h in range(H):
                ipart[h, o] = dot3(zh, zl, vh[h * W:(h + 1) * W, :], vl[h * W:(h + 1) * W, :], ((1,), (1,)))

                @pl.when(jnp.logical_and(ma == 0, o > 0))
                def _():
                    i_copy(h, o, True).start()

                @pl.when(jnp.logical_and(ma == A - 1, o < A - 1))
                def _():
                    i_copy(h, o, False).start()

    def i_relay(e):
        blocks = [slab * nb + (e if 2 * slab < m else nb - 1 - e) for slab in range(m)]
        pairs = list(inward(blocks))
        for step in range(0, len(pairs), 2):
            for h in range(H):
                for o, up in pairs[step:step + 2]:
                    inner, first = (ma < o, ma > 0) if up else (ma > o, ma < A - 1)

                    @pl.when(jnp.logical_and(inner, first))
                    def _(h=h, o=o, up=up):
                        i_copy(h, o, up).wait_recv()
                        ipart[h, o] = ipart[h, o] + (iup if up else idown)[h, o]
                        i_copy(h, o, up).start()

    def start_values():
        v_own().start()
        for k in range(2, B, 2):
            v_copy(k).start()

    def pass_values():
        for k in range(2, B, 2):
            v_arrival(b_peer(k)).wait_recv()
            v_pass(k).start()

    def take_values():
        v_arrival(twin).wait_recv()
        for k in range(2, B, 2):
            v_arrival(lax.rem(twin + k, B)).wait_recv()
        for j in range(B):
            high, low = split(vbuf[j])
            vh[:, j * S:(j + 1) * S] = high
            vl[:, j * S:(j + 1) * S] = low

    z_parts(0)
    start_values()
    for e in range(nb):
        z_relay(e)
        if e + 1 < nb:
            z_parts(e + 1)
        if e == 0:
            pass_values()
        if e:
            i_parts(e - 1)
        else:
            take_values()
        z_sum(e)
        if e:
            i_relay(e - 1)
    i_parts(nb - 1)
    i_relay(nb - 1)
    W = out_ref.shape[1] // H
    for h in range(H):
        out_ref[:, h * W:(h + 1) * W] = own_sum(i_copy, ipart, iup, idown, h)

    for k in range(1, n):
        coord_copy(k).wait_send()
    for e in range(nb):
        for k in range(1, B):
            g_copy(e, k).wait_send()
        for k in range(1, m):
            x_copy(e, k).wait_send()
    v_own().wait_send()
    for k in range(2, B, 2):
        v_copy(k).wait_send()
        v_pass(k).wait_send()
    for o in range(A):
        @pl.when(o != ma)
        def _(o=o):
            for e in range(nb):
                z_copy(e, o, True).wait_send()
            for h in range(H):
                i_copy(h, o, True).wait_send()


def solution(mesh):
    n, m = mesh.shape["grid"], mesh.shape["vec"]
    A = min((d for d in range(m, n + 1, m) if n % d == 0), key=lambda d: abs(d - n // d))
    B, nb = n // A, A // m

    def body(tgt_coords, src_coords, src_values, grad_vectors):
        T, S = tgt_coords.shape[1], src_coords.shape[1]
        Q, slab = src_values.shape[0], grad_vectors.shape[1]
        R = slab * m // n
        f32, bf16 = jnp.float32, jnp.bfloat16
        coords = jnp.concatenate([src_coords, tgt_coords, jnp.zeros((2, S), f32)], axis=0)
        grads = grad_vectors.reshape(3, nb, B, R, T)
        depth, width = 3 * B * T, B * S
        H = 2 if Q % 256 == 0 else 1
        slots = max(1, min(A, K_BYTES // (depth * width * 4)))
        V, DMA = pltpu.VMEM, pltpu.SemaphoreType.DMA
        return pl.pallas_call(
            functools.partial(kernel, (A, B, m, nb, R, T, S, H, slots)),
            out_shape=jax.ShapeDtypeStruct((R, Q), f32),
            in_specs=[pl.BlockSpec(memory_space=pltpu.VMEM)] * 3,
            out_specs=pl.BlockSpec(memory_space=pltpu.VMEM),
            scratch_shapes=[
                V((n, 8, S), f32), V((3, B * T, S), f32),
                V((nb, B, 3, R, T), f32), V((R, depth), bf16), V((R, depth), bf16),
                V((B, Q, S), f32), V((Q, width), bf16), V((Q, width), bf16),
                V((slots, depth, width), bf16), V((slots, depth, width), bf16),
                V((nb, A, R, width), f32), V((nb, A, R, width), f32), V((nb, A, R, width), f32),
                V((nb, m, R, width), f32),
                V((H, A, R, Q // H), f32), V((H, A, R, Q // H), f32), V((H, A, R, Q // H), f32),
                DMA((n,)), DMA((n,)), DMA((nb, B)), DMA((nb, B)), DMA((B,)), DMA((B,)),
                DMA((nb, A)), DMA((nb, A)), DMA((nb, A)), DMA((nb, m)), DMA((nb, m)),
                DMA((H, A)), DMA((H, A)), DMA((H, A)),
            ],
            compiler_params=pltpu.CompilerParams(
                collective_id=0, has_side_effects=True, vmem_limit_bytes=56 << 20),
        )(coords, src_values, grads)

    return jax.shard_map(
        body,
        mesh=mesh,
        in_specs=(P(None, "grid"), P(None, "grid"), P("vec", "grid"), P(None, "vec", "grid")),
        out_specs=P("grid", "vec"),
        check_vma=False,
    )
```

```python
import functools

import jax
import jax.numpy as jnp
from jax import lax
from jax.experimental import pallas as pl
from jax.experimental.pallas import tpu as pltpu
from jax.sharding import PartitionSpec as P

stiff = 1.0
soft = 0.05
MESH = pl.DeviceIdType.MESH
ROWS = 16
K_BYTES = 16 << 20


def split(value):
    high = value.astype(jnp.bfloat16)
    low = (value - high.astype(jnp.float32)).astype(jnp.bfloat16)
    return high, low


def dot3(ah, al, bh, bl, dims):
    dot = functools.partial(lax.dot_general, dimension_numbers=(dims, ((), ())), preferred_element_type=jnp.float32)
    return dot(ah, bh) + (dot(ah, bl) + dot(al, bh))


def kernel(sizes, coord_ref, v_ref, g_ref, out_ref,
           cbuf, tcol, gbuf, gh, gl, vbuf, vh, vl, kh, kl, zpart, zup, zdown, zall, ipart, iup, idown,
           csend, crecv, gsend, grecv, vsend, vrecv, zsend, zuprecv, zdownrecv, xsend, xrecv,
           isend, iuprecv, idownrecv):
    A, B, m, nb, R, T, S, H, slots = sizes
    n = A * B
    me, mv = lax.axis_index("grid"), lax.axis_index("vec")
    ma, mb = me // B, me % B

    barrier = pltpu.get_barrier_semaphore()
    for k in range(1, n):
        pl.semaphore_signal(barrier, inc=1, device_id={"grid": lax.rem(me + k, n)}, device_id_type=MESH)
    for k in range(1, m):
        pl.semaphore_signal(barrier, inc=1, device_id={"vec": lax.rem(mv + k, m)}, device_id_type=MESH)
    pl.semaphore_wait(barrier, n - 1 + m - 1)

    def remote(src, dst, send, recv, device):
        return pltpu.make_async_remote_copy(
            src_ref=src, dst_ref=dst, send_sem=send, recv_sem=recv, device_id=device, device_id_type=MESH)

    def coord_copy(k):
        return remote(coord_ref, cbuf.at[me], csend.at[k], crecv.at[me], {"grid": lax.rem(me + k, n)})

    def coord_arrival(k):
        o = lax.rem(me + k, n)
        return remote(coord_ref, cbuf.at[o], csend.at[k], crecv.at[o], {"grid": o})

    def b_peer(k):
        return lax.rem(mb + k, B)

    def row_block(e, slab):
        return jnp.where(2 * slab < m, e, nb - 1 - e)

    def g_copy(e, k):
        o = b_peer(k)
        return remote(g_ref.at[:, row_block(e, mv), o], gbuf.at[e, mb], gsend.at[e, k], grecv.at[e, mb],
                      {"grid": ma * B + o})

    def g_arrival(e, k):
        o = b_peer(k)
        return remote(gbuf.at[e, o], gbuf.at[e, o], gsend.at[e, k], grecv.at[e, o], {"grid": ma * B + o})

    twin = mb + 1 - 2 * lax.rem(mb, 2)

    def v_copy(k):
        return remote(v_ref, vbuf.at[mb], vsend.at[k], vrecv.at[mb], {"grid": ma * B + b_peer(k)})

    def v_pass(k):
        o = b_peer(k)
        return remote(vbuf.at[o], vbuf.at[o], vsend.at[k + 1], vrecv.at[o], {"grid": ma * B + twin})

    def v_own():
        return remote(v_ref, vbuf.at[mb], vsend.at[0], vrecv.at[mb], {"grid": ma * B + twin})

    def v_arrival(o):
        return remote(v_ref, vbuf.at[o], vsend.at[0], vrecv.at[o], {"grid": ma * B + twin})

    def z_copy(e, o, up):
        buf, recv, to = (zup, zuprecv, ma + 1) if up else (zdown, zdownrecv, ma - 1)
        return remote(zpart.at[e, o], buf.at[e, o], zsend.at[e, o], recv.at[e, o],
                      {"grid": lax.rem(to + A, A) * B + mb})

    def x_copy(e, k):
        return remote(zall.at[e, mv], zall.at[e, mv], xsend.at[e, k], xrecv.at[e, mv], {"vec": lax.rem(mv + k, m)})

    def x_arrival(e, k):
        o = lax.rem(mv + k, m)
        return remote(zall.at[e, o], zall.at[e, o], xsend.at[e, k], xrecv.at[e, o], {"vec": o})

    def i_copy(h, o, up):
        buf, recv, to = (iup, iuprecv, ma + 1) if up else (idown, idownrecv, ma - 1)
        return remote(ipart.at[h, o], buf.at[h, o], isend.at[h, o], recv.at[h, o],
                      {"grid": lax.rem(to + A, A) * B + mb})

    def inward(blocks):
        for u, d in zip(sorted(blocks, reverse=True), sorted(blocks)):
            yield u, True
            yield d, False

    for k in range(1, n):
        coord_copy(k).start()
    for e in range(nb):
        for k in range(1, B):
            g_copy(e, k).start()

    v_own().start()
    for k in range(2, B, 2):
        v_copy(k).start()

    cbuf[me] = coord_ref[...]
    for e in range(nb):
        gbuf[e, mb] = g_ref[:, row_block(e, mv), mb]
    vbuf[mb] = v_ref[...]

    for k in range(1, n):
        coord_arrival(k).wait_recv()

    for j in range(B):
        for c in range(3):
            row = cbuf[ma * B + j, 3 + c:4 + c, :]
            tcol[c, j * T:(j + 1) * T, :] = jnp.broadcast_to(row, (S, T)).T

    def make_pair_kernel(block, slot):
        def rows(i, carry):
            j, start = i // (T // ROWS), i % (T // ROWS) * ROWS
            at = pl.ds(pl.multiple_of(i * ROWS, ROWS), ROWS)
            txyz = [tcol[c, at, :] for c in range(3)]
            for q in range(B):
                src = block * B + q
                diff = [t - jnp.broadcast_to(cbuf[src, c:c + 1, :], (ROWS, S)) for c, t in enumerate(txyz)]
                dist2 = diff[0] * diff[0] + diff[1] * diff[1] + diff[2] * diff[2]
                near = 1.0 + stiff * jnp.sqrt(dist2)
                scale = 0.5 / (near * near * jnp.sqrt(dist2 + soft * soft))
                for c in range(3):
                    high, low = split(diff[c] * scale)
                    where = pl.ds(pl.multiple_of((j * 3 + c) * T + start, ROWS), ROWS)
                    kh[slot, where, q * S:(q + 1) * S] = high
                    kl[slot, where, q * S:(q + 1) * S] = low
            return carry
        lax.fori_loop(0, B * T // ROWS, rows, 0)

    order = []
    for u, d in zip(range(A - 1, -1, -1), range(A)):
        order += [o for o in (u, d) if o not in order]
    early = min(slots, 2)
    for slot in range(early):
        make_pair_kernel(order[slot], slot)

    def z_parts(e):
        for k in range(1, B):
            g_arrival(e, k).wait_recv()
        for j in range(B):
            for c in range(3):
                high, low = split(gbuf[e, j, c])
                gh[:, (j * 3 + c) * T:(j * 3 + c + 1) * T] = high
                gl[:, (j * 3 + c) * T:(j * 3 + c + 1) * T] = low
        for step, o in enumerate(order):
            slot = step % slots
            if (slots < A and e) or (e == 0 and step >= early):
                make_pair_kernel(o, slot)
            zpart[e, o] = dot3(gh[...], gl[...], kh[slot], kl[slot], ((1,), (0,)))

            @pl.when(jnp.logical_and(ma == 0, o > 0))
            def _():
                z_copy(e, o, True).start()

            @pl.when(jnp.logical_and(ma == A - 1, o < A - 1))
            def _():
                z_copy(e, o, False).start()

    def z_relay(e):
        for o, up in inward(range(A)):
            inner, first = (ma < o, ma > 0) if up else (ma > o, ma < A - 1)

            @pl.when(jnp.logical_and(inner, first))
            def _(o=o, up=up):
                z_copy(e, o, up).wait_recv()
                zpart[e, o] = zpart[e, o] + (zup if up else zdown)[e, o]
                z_copy(e, o, up).start()

    def own_sum(copy, part, upbuf, downbuf, h):
        @pl.when(ma > 0)
        def _():
            copy(h, ma, True).wait_recv()
            part[h, ma] = part[h, ma] + upbuf[h, ma]

        @pl.when(ma < A - 1)
        def _():
            copy(h, ma, False).wait_recv()
            part[h, ma] = part[h, ma] + downbuf[h, ma]
        return part[h, ma]

    def z_sum(e):
        zall[e, mv] = own_sum(z_copy, zpart, zup, zdown, e)
        for k in range(1, m):
            x_copy(e, k).start()

    def i_parts(e):
        for k in range(1, m):
            x_arrival(e, k).wait_recv()
        blocks = {slab * nb + (e if 2 * slab < m else nb - 1 - e): slab for slab in range(m)}
        W = vh.shape[0] // H
        for o in sorted(blocks, key=order.index):
            zh, zl = split(zall[e, blocks[o]])
            for h in range(H):
                ipart[h, o] = dot3(zh, zl, vh[h * W:(h + 1) * W, :], vl[h * W:(h + 1) * W, :], ((1,), (1,)))

                @pl.when(jnp.logical_and(ma == 0, o > 0))
                def _():
                    i_copy(h, o, True).start()

                @pl.when(jnp.logical_and(ma == A - 1, o < A - 1))
                def _():
                    i_copy(h, o, False).start()

    def i_relay(e):
        blocks = [slab * nb + (e if 2 * slab < m else nb - 1 - e) for slab in range(m)]
        pairs = list(inward(blocks))
        for step in range(0, len(pairs), 2):
            for h in range(H):
                for o, up in pairs[step:step + 2]:
                    inner, first = (ma < o, ma > 0) if up else (ma > o, ma < A - 1)

                    @pl.when(jnp.logical_and(inner, first))
                    def _(h=h, o=o, up=up):
                        i_copy(h, o, up).wait_recv()
                        ipart[h, o] = ipart[h, o] + (iup if up else idown)[h, o]
                        i_copy(h, o, up).start()

    def pass_values():
        for k in range(2, B, 2):
            v_arrival(b_peer(k)).wait_recv()
            v_pass(k).start()

    def take_values():
        v_arrival(twin).wait_recv()
        for k in range(2, B, 2):
            v_arrival(lax.rem(twin + k, B)).wait_recv()
        for j in range(B):
            high, low = split(vbuf[j])
            vh[:, j * S:(j + 1) * S] = high
            vl[:, j * S:(j + 1) * S] = low

    z_parts(0)
    for e in range(nb):
        if e != 1:
            z_relay(e)
        if e + 1 < nb:
            z_parts(e + 1)
        if e:
            i_parts(e - 1)
        z_sum(e)
        if e == 0:
            pass_values()
            if nb > 1:
                z_relay(1)
            take_values()
        if e:
            i_relay(e - 1)
    i_parts(nb - 1)
    i_relay(nb - 1)
    W = out_ref.shape[1] // H
    for h in range(H):
        out_ref[:, h * W:(h + 1) * W] = own_sum(i_copy, ipart, iup, idown, h)

    for k in range(1, n):
        coord_copy(k).wait_send()
    for e in range(nb):
        for k in range(1, B):
            g_copy(e, k).wait_send()
        for k in range(1, m):
            x_copy(e, k).wait_send()
    v_own().wait_send()
    for k in range(2, B, 2):
        v_copy(k).wait_send()
        v_pass(k).wait_send()
    for o in range(A):
        @pl.when(o != ma)
        def _(o=o):
            for e in range(nb):
                z_copy(e, o, True).wait_send()
            for h in range(H):
                i_copy(h, o, True).wait_send()


def solution(mesh):
    n, m = mesh.shape["grid"], mesh.shape["vec"]
    A = min((d for d in range(m, n + 1, m) if n % d == 0), key=lambda d: abs(d - n // d))
    B, nb = n // A, A // m

    def body(tgt_coords, src_coords, src_values, grad_vectors):
        T, S = tgt_coords.shape[1], src_coords.shape[1]
        Q, slab = src_values.shape[0], grad_vectors.shape[1]
        R = slab * m // n
        f32, bf16 = jnp.float32, jnp.bfloat16
        coords = jnp.concatenate([src_coords, tgt_coords, jnp.zeros((2, S), f32)], axis=0)
        grads = grad_vectors.reshape(3, nb, B, R, T)
        depth, width = 3 * B * T, B * S
        H = 2 if Q % 256 == 0 else 1
        slots = max(1, min(A, K_BYTES // (depth * width * 4)))
        V, DMA = pltpu.VMEM, pltpu.SemaphoreType.DMA
        return pl.pallas_call(
            functools.partial(kernel, (A, B, m, nb, R, T, S, H, slots)),
            out_shape=jax.ShapeDtypeStruct((R, Q), f32),
            in_specs=[pl.BlockSpec(memory_space=pltpu.VMEM)] * 3,
            out_specs=pl.BlockSpec(memory_space=pltpu.VMEM),
            scratch_shapes=[
                V((n, 8, S), f32), V((3, B * T, S), f32),
                V((nb, B, 3, R, T), f32), V((R, depth), bf16), V((R, depth), bf16),
                V((B, Q, S), f32), V((Q, width), bf16), V((Q, width), bf16),
                V((slots, depth, width), bf16), V((slots, depth, width), bf16),
                V((nb, A, R, width), f32), V((nb, A, R, width), f32), V((nb, A, R, width), f32),
                V((nb, m, R, width), f32),
                V((H, A, R, Q // H), f32), V((H, A, R, Q // H), f32), V((H, A, R, Q // H), f32),
                DMA((n,)), DMA((n,)), DMA((nb, B)), DMA((nb, B)), DMA((B,)), DMA((B,)),
                DMA((nb, A)), DMA((nb, A)), DMA((nb, A)), DMA((nb, m)), DMA((nb, m)),
                DMA((H, A)), DMA((H, A)), DMA((H, A)),
            ],
            compiler_params=pltpu.CompilerParams(
                collective_id=0, has_side_effects=True, vmem_limit_bytes=56 << 20),
        )(coords, src_values, grads)

    return jax.shard_map(
        body,
        mesh=mesh,
        in_specs=(P(None, "grid"), P(None, "grid"), P("vec", "grid"), P(None, "vec", "grid")),
        out_specs=P("grid", "vec"),
        check_vma=False,
    )
```
